768 devices in a mesh: gx: 4 (over x_lo, core), gy: 12 (over z), gz: 16 (over y, x_hi).
Axes of the slice: x: 4 (x_hi: 2, x_lo: 2; x = x_hi * 2 + x_lo), y: 8, z: 12, core: 2. Of those that a mesh axis runs over, the one named last changes fastest.
Arguments:
- gauge_links: float32 [4, 3, 3, 2, 8, 24, 16, 128], P(None, None, None, None, 'gx', 'gy', 'gz'), may hold values from -1 to 1, as said below
- momenta: float32 [4, 3, 3, 2, 8, 24, 16, 128], P(None, None, None, None, 'gx', 'gy', 'gz'), may hold values from -6 to 6, as said below
Outputs:
- new_links: float32 [4, 3, 3, 2, 8, 24, 16, 128], P(None, None, None, None, 'gx', 'gy', 'gz')
- new_momenta: float32 [4, 3, 3, 2, 8, 24, 16, 128], P(None, None, None, None, 'gx', 'gy', 'gz')
The draws below stay inside these ranges and needn't reach their ends.
Inputs may be any that keep to these rules, and one draw needn't show every extreme that they name: `gauge_links`: every link is a unitary 3 x 3 matrix of determinant one. `momenta`: every momentum is an anti-Hermitian 3 x 3 matrix of trace zero.
All inputs are finite; a program needn't handle non-finite values.
Results may differ from the reference program's by a relative error of at most 0.0001.
Values sent between devices are 32-bit elements; how exact they have to be, the bound alone decides.
No kernel may reach another device: no remote copies, remote signals or barrier semaphores. Data moves between devices by JAX's collectives and lax.ppermute only.
A program may use at most 32 MiB of HBM per device.

```python
import math
import jax
import jax.numpy as jnp

NT = 128
NX = 8
NY = 24
NZ = 16


def product_drawn(left, right):
    left_real = left[:, :, 0]
    left_imag = left[:, :, 1]
    right_real = right[:, :, 0]
    right_imag = right[:, :, 1]
    real_part = jnp.sum(left_real[:, :, None] * right_real[None] - left_imag[:, :, None] * right_imag[None], axis=1)
    imag_part = jnp.sum(left_real[:, :, None] * right_imag[None] + left_imag[:, :, None] * right_real[None], axis=1)
    return jnp.stack([real_part, imag_part], axis=2)


def assemble(real_rows, imag_rows):
    return jnp.stack([jnp.stack([jnp.stack([real_rows[row_index][column_index], imag_rows[row_index][column_index]]) for column_index in range(3)]) for row_index in range(3)])


def rotation(rotation_angle, height, azimuth, first, second):
    cosine = jnp.cos(rotation_angle)
    sine = jnp.sin(rotation_angle)
    lateral = jnp.sqrt(1.0 - height * height)
    comp_one = sine * lateral * jnp.cos(azimuth)
    comp_two = sine * lateral * jnp.sin(azimuth)
    comp_three = sine * height
    zeros = jnp.zeros_like(cosine)
    ones = jnp.ones_like(cosine)
    third = 3 - first - second
    real_rows = [[zeros, zeros, zeros] for unused_row in range(3)]
    imag_rows = [[zeros, zeros, zeros] for unused_row in range(3)]
    real_rows[first][first] = cosine
    imag_rows[first][first] = comp_three
    real_rows[first][second] = comp_two
    imag_rows[first][second] = comp_one
    real_rows[second][first] = -comp_two
    imag_rows[second][first] = comp_one
    real_rows[second][second] = cosine
    imag_rows[second][second] = -comp_three
    real_rows[third][third] = ones
    return assemble(real_rows, imag_rows)


def draw_gauge_links(key, part):
    extent = (4, NX, NY, NZ, NT)
    keys = jax.random.split(key, 9)
    highest = math.pi
    pairs = ((0, 1), (1, 2), (0, 2))
    running = None
    for number in range(3):
        rotation_angle = jax.random.uniform(keys[3 * number], extent, jnp.float32, 0.0, highest)
        height = jax.random.uniform(keys[3 * number + 1], extent, jnp.float32, -1.0, 1.0)
        azimuth = jax.random.uniform(keys[3 * number + 2], extent, jnp.float32, -math.pi, math.pi)
        factor = rotation(rotation_angle, height, azimuth, pairs[number][0], pairs[number][1])
        running = factor if number == 0 else product_drawn(running, factor)
    return jnp.moveaxis(running, 3, 0).astype(jnp.float32)


def draw_momenta(key, part):
    extent = (8, 4, NX, NY, NZ, NT)
    values = jax.random.truncated_normal(key, -3.0, 3.0, extent, jnp.float32)
    zeros = jnp.zeros_like(values[0])
    diag_one = values[0]
    diag_two = values[1]
    diag_three = -diag_one - diag_two
    real_rows = [[zeros, -values[5], -values[6]], [values[5], zeros, -values[7]], [values[6], values[7], zeros]]
    imag_rows = [[diag_one, values[2], values[3]], [values[2], diag_two, values[4]], [values[3], values[4], diag_three]]
    matrix = assemble(real_rows, imag_rows)
    return jnp.moveaxis(matrix, 3, 0).astype(jnp.float32)


def setup_inputs(seed: int = 0) -> dict:
    key_of = jax.random.split(jax.random.key(seed), 3)
    gauge_links = draw_gauge_links(jax.random.fold_in(key_of[2], 71), 0)
    momenta = draw_momenta(jax.random.fold_in(key_of[2], 71), 0)
    return {"gauge_links": gauge_links, "momenta": momenta}


BETA = 5.7
STEP = 0.25


def product(left, right):
    left_real = left[:, :, 0]
    left_imag = left[:, :, 1]
    right_real = right[:, :, 0]
    right_imag = right[:, :, 1]
    real_part = jnp.sum(left_real[:, :, None] * right_real[None] - left_imag[:, :, None] * right_imag[None], axis=1)
    imag_part = jnp.sum(left_real[:, :, None] * right_imag[None] + left_imag[:, :, None] * right_real[None], axis=1)
    return jnp.stack([real_part, imag_part], axis=2)


def dagger(matrix):
    return jnp.stack([jnp.swapaxes(matrix[:, :, 0], 0, 1), -jnp.swapaxes(matrix[:, :, 1], 0, 1)], axis=2)


def add_identity(matrix):
    identity = jnp.eye(3, dtype=jnp.float32).reshape((3, 3) + (1,) * (matrix.ndim - 3))
    return jnp.stack([matrix[:, :, 0] + identity, matrix[:, :, 1]], axis=2)


def exponent(generator):
    series = add_identity(generator / 4.0)
    series = add_identity(product(generator, series) / 3.0)
    series = add_identity(product(generator, series) / 2.0)
    return add_identity(product(generator, series))


def project(omega):
    real_part = 0.5 * (omega[:, :, 0] - jnp.swapaxes(omega[:, :, 0], 0, 1))
    imag_part = 0.5 * (omega[:, :, 1] + jnp.swapaxes(omega[:, :, 1], 0, 1))
    trace = (omega[0, 0, 1] + omega[1, 1, 1] + omega[2, 2, 1]) / 3.0
    identity = jnp.eye(3, dtype=jnp.float32).reshape((3, 3) + (1,) * trace.ndim)
    imag_part = imag_part - identity * trace
    return jnp.stack([real_part, imag_part], axis=2)


def move(matrix, direction, amount):
    return jnp.roll(matrix, -amount, axis=3 + direction)


def forces(field):
    result = []
    for along in range(4):
        running = jnp.zeros_like(field[along])
        for across in range(4):
            if across == along:
                continue
            upper = product(product(move(field[across], along, 1), dagger(move(field[along], across, 1))), dagger(field[across]))
            lower_site = product(product(dagger(move(field[across], along, 1)), dagger(field[along])), field[across])
            lower = move(lower_site, across, -1)
            running = running + upper + lower
        omega = product(field[along], running)
        result.append((BETA / 3.0) * project(omega))
    return result


def reference(gauge_links, momenta):
    field = [gauge_links[direction] for direction in range(4)]
    moment = [momenta[direction] for direction in range(4)]
    kick = forces(field)
    moment = [moment[direction] - (0.5 * STEP) * kick[direction] for direction in range(4)]
    for repeat in range(2):
        field = [product(exponent(STEP * moment[direction]), field[direction]) for direction in range(4)]
        kick = forces(field)
        factor = STEP if repeat == 0 else 0.5 * STEP
        moment = [moment[direction] - factor * kick[direction] for direction in range(4)]
    return jnp.stack(field), jnp.stack(moment)
```

```python
import functools

import jax
import jax.numpy as jnp
from jax import lax
from jax.experimental import pallas as pl
from jax.experimental.pallas import tpu as pltpu
from jax.sharding import PartitionSpec as P

BETA = 5.7
STEP = 0.25
F32 = jnp.float32

OTHERS = ((1, 2, 3), (0, 2, 3), (0, 1, 3))
PLANES = ((0, 1), (0, 2), (0, 3), (1, 2), (1, 3), (2, 3))
PAIRS = ((0, 1), (0, 2), (1, 2))


def mat(ref, base):
    return [[(ref[base + 6 * i + 2 * j], ref[base + 6 * i + 2 * j + 1]) for j in range(3)] for i in range(3)]


def put(ref, base, m):
    for i in range(3):
        for j in range(3):
            ref[base + 6 * i + 2 * j] = m[i][j][0]
            ref[base + 6 * i + 2 * j + 1] = m[i][j][1]


def dag(m):
    return [[(m[j][i][0], -m[j][i][1]) for j in range(3)] for i in range(3)]


def total(terms):
    out = terms[0]
    for t in terms[1:]:
        out = out + t
    return out


def re_dot(a, b, ca, cb):
    if ca == cb:
        return total([x[0] * y[0] - x[1] * y[1] for x, y in zip(a, b)])
    return total([x[0] * y[0] + x[1] * y[1] for x, y in zip(a, b)])


def im_dot(a, b, ca, cb):
    if not ca and not cb:
        return total([x[0] * y[1] + x[1] * y[0] for x, y in zip(a, b)])
    if ca and not cb:
        return total([x[0] * y[1] - x[1] * y[0] for x, y in zip(a, b)])
    if cb and not ca:
        return total([x[1] * y[0] - x[0] * y[1] for x, y in zip(a, b)])
    return -total([x[0] * y[1] + x[1] * y[0] for x, y in zip(a, b)])


def row(m, i, d):
    return [m[k][i] for k in range(3)] if d else [m[i][k] for k in range(3)]


def col(m, j, d):
    return [m[j][k] for k in range(3)] if d else [m[k][j] for k in range(3)]


def mul(a, b, da=False, db=False):
    return [
        [(re_dot(row(a, i, da), col(b, j, db), da, db), im_dot(row(a, i, da), col(b, j, db), da, db)) for j in range(3)]
        for i in range(3)
    ]


def anti(a, b, da=False, db=False):
    out = []
    for i, j in PAIRS:
        ri, cj, rj, ci = row(a, i, da), col(b, j, db), row(a, j, da), col(b, i, db)
        out.append(re_dot(ri, cj, da, db) - re_dot(rj, ci, da, db))
        out.append(im_dot(ri, cj, da, db) + im_dot(rj, ci, da, db))
    for i in range(3):
        out.append(im_dot(row(a, i, da), col(b, i, db), da, db))
    return out


def expand(h):
    m = [[None] * 3 for _ in range(3)]
    for n, (i, j) in enumerate(PAIRS):
        m[i][j] = (h[2 * n], h[2 * n + 1])
        m[j][i] = (-h[2 * n], h[2 * n + 1])
    for i in range(3):
        m[i][i] = (None, h[6 + i])
    return m


def step_x(own, halo):
    return jnp.concatenate([own[2:4], halo], axis=0)


def step_y(own, halo):
    return jnp.concatenate([own[1:2], halo[0:1], own[3:4], halo[1:2]], axis=0)


def back_x(own, halo):
    return jnp.concatenate([halo, own[0:2]], axis=0)


def back_y(own, halo):
    return jnp.concatenate([halo[0:1], own[0:1], halo[1:2], own[2:3]], axis=0)


def faces(u_ref, mz, my, mx):
    for n, d in enumerate(OTHERS[2]):
        for c in range(18):
            mz[18 * n + c] = u_ref[18 * d + c]
    for n, d in enumerate(OTHERS[1]):
        for c in range(18):
            my[18 * n + c, 0:1] = u_ref[18 * d + c, 0:1]
            my[18 * n + c, 1:2] = u_ref[18 * d + c, 2:3]
    for n, d in enumerate(OTHERS[0]):
        for c in range(18):
            mx[18 * n + c] = u_ref[18 * d + c, 0:2]


def first_kernel(u_ref, mz, my, mx):
    faces(u_ref, mz, my, mx)


def local_kernel(u_ref, r_ref):
    for n, (mu, nu) in enumerate(PLANES):
        put(r_ref, 18 * n, mul(mat(u_ref, 18 * mu), mat(u_ref, 18 * nu), da=True))


def lower_kernel(u_ref, r_ref, rz, ry, rx, tz, ty, tx, sx, sy, st, own_x, own_y, own_t):
    for n, d in enumerate(OTHERS[0]):
        for c in range(18):
            sx[18 * n + c] = step_x(u_ref[18 * d + c], rx[18 * n + c])
    for n, d in enumerate(OTHERS[1]):
        for c in range(18):
            sy[18 * n + c] = step_y(u_ref[18 * d + c], ry[18 * n + c])
    for d in range(3):
        for c in range(18):
            st[18 * d + c] = pltpu.roll(u_ref[18 * d + c], 127, 1)
    moved = (sx, sy, rz, st)

    def at(direction, axis):
        where = OTHERS[axis].index(direction) if axis < 3 else direction
        return mat(moved[axis], 18 * where)

    lows = (own_x, own_y, tz, own_t)
    for n, (mu, nu) in enumerate(PLANES):
        q = mul(at(mu, nu), at(nu, mu), db=True)
        r = mat(r_ref, 18 * n)
        for along, across, d in ((mu, nu, False), (nu, mu, True)):
            where = OTHERS[across].index(along) if across < 3 else along
            for c, v in enumerate(anti(q, r, da=d, db=d)):
                lows[across][9 * where + c] = v
    for k in range(27):
        ty[k, 0:1] = own_y[k, 1:2]
        ty[k, 1:2] = own_y[k, 3:4]
        tx[k] = own_x[k, 2:4]


def upper_kernel(u_ref, rz, sx, sy, st, own_t, f_ref):
    moved = (sx, sy, rz, st)

    def at(direction, axis):
        where = OTHERS[axis].index(direction) if axis < 3 else direction
        return mat(moved[axis], 18 * where)

    for k in range(27):
        f_ref[k] = pltpu.roll(own_t[k], 1, 1)
    for k in range(9):
        f_ref[27 + k] = jnp.zeros((4, 128), F32)
    for mu, nu in PLANES:
        first = mul(mat(u_ref, 18 * mu), at(nu, mu))
        second = mul(mat(u_ref, 18 * nu), at(mu, nu))
        for c, v in enumerate(anti(first, second, db=True)):
            f_ref[9 * mu + c] = f_ref[9 * mu + c] + v
            f_ref[9 * nu + c] = f_ref[9 * nu + c] - v


def force_of(d, f_ref, tz, ty, tx, own_x, own_y):
    out = []
    for c in range(9):
        v = f_ref[9 * d + c]
        if d != 0:
            k = 9 * OTHERS[0].index(d) + c
            v = v + back_x(own_x[k], tx[k])
        if d != 1:
            k = 9 * OTHERS[1].index(d) + c
            v = v + back_y(own_y[k], ty[k])
        if d != 2:
            k = 9 * OTHERS[2].index(d) + c
            v = v + tz[k]
        out.append(v)
    mean = (out[6] + out[7] + out[8]) * (1.0 / 3.0)
    return [0.5 * v for v in out[:6]] + [v - mean for v in out[6:]]


def read_momenta(p_ref, d, full):
    if not full:
        return [p_ref[9 * d + c] for c in range(9)]
    out = []
    for i, j in PAIRS:
        out += [p_ref[18 * d + 6 * i + 2 * j], p_ref[18 * d + 6 * i + 2 * j + 1]]
    return out + [p_ref[18 * d + 8 * i + 1] for i in range(3)]


def square(x):
    h = [[None] * 3 for _ in range(3)]
    m = expand(x)
    for i in range(3):
        for j in range(i, 3):
            re, im = [], []
            for k in range(3):
                a, b = m[i][k], m[k][j]
                if a[0] is not None and b[0] is not None:
                    re.append(a[0] * b[0])
                re.append(-(a[1] * b[1]))
                if a[0] is not None:
                    im.append(a[0] * b[1])
                if b[0] is not None:
                    im.append(a[1] * b[0])
            h[i][j] = (total(re), total(im) if i != j else None)
            if i != j:
                h[j][i] = (h[i][j][0], -h[i][j][1])
    return h


def exponent(x):
    h, m = square(x), expand(x)
    k = [[None] * 3 for _ in range(3)]
    for i in range(3):
        for j in range(3):
            if i == j:
                k[i][j] = (h[i][j][0] * (1.0 / 24.0) + 0.5, m[i][j][1] * (1.0 / 6.0))
            else:
                k[i][j] = tuple(h[i][j][c] * (1.0 / 24.0) + m[i][j][c] * (1.0 / 6.0) for c in range(2))
    e = [[None] * 3 for _ in range(3)]
    for i in range(3):
        for j in range(3):
            re, im = [], []
            for n in range(3):
                a, b = h[i][n], k[n][j]
                re.append(a[0] * b[0])
                im.append(a[0] * b[1])
                if a[1] is not None:
                    re.append(-(a[1] * b[1]))
                    im.append(a[1] * b[0])
            re, im = total(re), total(im)
            if i == j:
                e[i][j] = (re + 1.0, im + m[i][j][1])
            else:
                e[i][j] = (re + m[i][j][0], im + m[i][j][1])
    return e


def drift_kernel(factor, full, u_ref, p_ref, f_ref, tz, ty, tx, own_x, own_y, q_ref, v_ref, mz, my, mx):
    for d in range(4):
        force = force_of(d, f_ref, tz, ty, tx, own_x, own_y)
        p = [a - (factor * BETA / 3.0) * b for a, b in zip(read_momenta(p_ref, d, full), force)]
        for c in range(9):
            q_ref[9 * d + c] = p[c]
        put(v_ref, 18 * d, mul(exponent([STEP * a for a in p]), mat(u_ref, 18 * d)))
    faces(v_ref, mz, my, mx)


def last_kernel(factor, p_ref, f_ref, tz, ty, tx, own_x, own_y, q_ref):
    for d in range(4):
        force = force_of(d, f_ref, tz, ty, tx, own_x, own_y)
        p = [a - (factor * BETA / 3.0) * b for a, b in zip(read_momenta(p_ref, d, False), force)]
        m = expand(p)
        for i in range(3):
            for j in range(3):
                re = jnp.zeros((4, 128), F32) if m[i][j][0] is None else m[i][j][0]
                q_ref[18 * d + 6 * i + 2 * j] = re
                q_ref[18 * d + 6 * i + 2 * j + 1] = m[i][j][1]


def call(kernel, outs, name, products):
    vm = pl.BlockSpec(memory_space=pltpu.VMEM)

    def run(*args):
        size = sum(a.size for a in args) + sum(o[0] * o[1] * 128 for o in outs)
        return pl.pallas_call(
            kernel,
            out_shape=[jax.ShapeDtypeStruct((o[0], o[1], 128), F32) for o in outs],
            in_specs=[vm] * len(args),
            out_specs=[vm] * len(outs),
            name=name,
            cost_estimate=pl.CostEstimate(flops=products * 200 * 512, bytes_accessed=4 * size, transcendentals=0),
            compiler_params=pltpu.CompilerParams(vmem_limit_bytes=8 * 1024 * 1024),
        )(*args)

    return run


def shifted(value, axis, steps):
    count = lax.axis_size(axis)
    return lax.ppermute(value, axis, [(source, (source + steps) % count) for source in range(count)])


def exchange(z, y, x, steps):
    return shifted(z, "gz", steps), shifted(y, "gy", steps), shifted(x, "gx", steps)


FACES = ((54, 4), (54, 2), (54, 2))


def body(gauge_links, momenta):
    u = gauge_links.reshape(72, 4, 128)
    p = momenta.reshape(72, 4, 128)
    sent = call(first_kernel, FACES, "first", 1)(u)
    for repeat in range(3):
        rz, ry, rx = exchange(*sent, -1)
        r = call(local_kernel, ((108, 4),), "local", 6)(u)[0]
        tz, ty, tx, sx, sy, st, own_x, own_y, own_t = call(
            lower_kernel,
            ((27, 4), (27, 2), (27, 2), (54, 4), (54, 4), (54, 4), (27, 4), (27, 4), (27, 4)),
            "lower",
            18,
        )(u, r, rz, ry, rx)
        gz, gy, gx = exchange(tz, ty, tx, 1)
        f = call(upper_kernel, ((36, 4),), "upper", 18)(u, rz, sx, sy, st, own_t)[0]
        factor = STEP if repeat == 1 else 0.5 * STEP
        if repeat < 2:
            p, u, *sent = call(
                functools.partial(drift_kernel, factor, repeat == 0), ((36, 4), (72, 4)) + FACES, "drift", 16
            )(u, p, f, gz, gy, gx, own_x, own_y)
        else:
            p = call(functools.partial(last_kernel, factor), ((72, 4),), "last", 2)(p, f, gz, gy, gx, own_x, own_y)[0]
    shape = gauge_links.shape
    return u.reshape(shape), p.reshape(shape)


def solution(mesh):
    placed = P(None, None, None, None, "gx", "gy", "gz", None)
    return jax.shard_map(
        body, mesh=mesh, in_specs=(placed, placed), out_specs=(placed, placed), check_vma=False
    )
```

```python
import functools

import jax
import jax.numpy as jnp
from jax import lax
from jax.experimental import pallas as pl
from jax.experimental.pallas import tpu as pltpu
from jax.sharding import PartitionSpec as P


BETA = 5.7
STEP = 0.25
F32 = jnp.float32

OTHERS = ((1, 2, 3), (0, 2, 3), (0, 1, 3))
PLANES = ((0, 1), (0, 2), (0, 3), (1, 2), (1, 3), (2, 3))
PAIRS = ((0, 1), (0, 2), (1, 2))
INNER = ((1, 2), (2, 1), (1, 3), (3, 1), (2, 3), (3, 2))


def mat(ref, base):
    return [[(ref[base + 6 * i + 2 * j], ref[base + 6 * i + 2 * j + 1]) for j in range(3)] for i in range(3)]


def put(ref, base, m):
    for i in range(3):
        for j in range(3):
            ref[base + 6 * i + 2 * j] = m[i][j][0]
            ref[base + 6 * i + 2 * j + 1] = m[i][j][1]


def total(terms):
    out = terms[0]
    for t in terms[1:]:
        out = out + t
    return out


def re_dot(a, b, ca, cb):
    if ca == cb:
        return total([x[0] * y[0] - x[1] * y[1] for x, y in zip(a, b)])
    return total([x[0] * y[0] + x[1] * y[1] for x, y in zip(a, b)])


def im_dot(a, b, ca, cb):
    if not ca and not cb:
        return total([x[0] * y[1] + x[1] * y[0] for x, y in zip(a, b)])
    if ca and not cb:
        return total([x[0] * y[1] - x[1] * y[0] for x, y in zip(a, b)])
    if cb and not ca:
        return total([x[1] * y[0] - x[0] * y[1] for x, y in zip(a, b)])
    return -total([x[0] * y[1] + x[1] * y[0] for x, y in zip(a, b)])


def row(m, i, d):
    return [m[k][i] for k in range(3)] if d else [m[i][k] for k in range(3)]


def col(m, j, d):
    return [m[j][k] for k in range(3)] if d else [m[k][j] for k in range(3)]


def mul(a, b, da=False, db=False):
    return [
        [(re_dot(row(a, i, da), col(b, j, db), da, db), im_dot(row(a, i, da), col(b, j, db), da, db)) for j in range(3)]
        for i in range(3)
    ]


def anti(a, b, da=False, db=False):
    out = []
    for i, j in PAIRS:
        ri, cj, rj, ci = row(a, i, da), col(b, j, db), row(a, j, da), col(b, i, db)
        out.append(re_dot(ri, cj, da, db) - re_dot(rj, ci, da, db))
        out.append(im_dot(ri, cj, da, db) + im_dot(rj, ci, da, db))
    for i in range(3):
        out.append(im_dot(row(a, i, da), col(b, i, db), da, db))
    return out


def expand(h):
    m = [[None] * 3 for _ in range(3)]
    for n, (i, j) in enumerate(PAIRS):
        m[i][j] = (h[2 * n], h[2 * n + 1])
        m[j][i] = (-h[2 * n], h[2 * n + 1])
    for i in range(3):
        m[i][i] = (None, h[6 + i])
    return m


def step_x(own, halo):
    return jnp.concatenate([own[2:4], halo], axis=0)


def step_y(own, halo):
    return jnp.concatenate([own[1:2], halo[0:1], own[3:4], halo[1:2]], axis=0)


def back_x(own, halo):
    return jnp.concatenate([halo, own[0:2]], axis=0)


def back_y(own, halo):
    return jnp.concatenate([halo[0:1], own[0:1], halo[1:2], own[2:3]], axis=0)


def face_z(u_ref, mz):
    for n, d in enumerate(OTHERS[2]):
        for c in range(18):
            mz[18 * n + c] = u_ref[18 * d + c]


def faces(u_ref, my, mx):
    for n, d in enumerate(OTHERS[1]):
        for c in range(18):
            my[18 * n + c, 0:1] = u_ref[18 * d + c, 0:1]
            my[18 * n + c, 1:2] = u_ref[18 * d + c, 2:3]
    for n, d in enumerate(OTHERS[0]):
        for c in range(18):
            mx[18 * n + c] = u_ref[18 * d + c, 0:2]


def first_kernel(u_ref, my, mx):
    faces(u_ref, my, mx)


def local_kernel(u_ref, r_ref, copy_ref=None):
    if copy_ref is not None:
        copy_ref[...] = u_ref[...]
    for n, (mu, nu) in enumerate(PLANES):
        put(r_ref, 18 * n, mul(mat(u_ref, 18 * mu), mat(u_ref, 18 * nu), da=True))


def reader(sx, sy, rz, st):
    def at(direction, axis):
        ref = (sx, sy, rz, st)[axis]
        where = direction if axis == 3 or ref.shape[0] == 72 else OTHERS[axis].index(direction)
        return mat(ref, 18 * where)

    return at


def lower_terms(planes, at, r_ref, out):
    for mu, nu in planes:
        q = mul(at(mu, nu), at(nu, mu), db=True)
        r = mat(r_ref, 18 * PLANES.index((mu, nu)))
        for along, across, d in ((mu, nu, False), (nu, mu, True)):
            for c, v in enumerate(anti(q, r, da=d, db=d)):
                out(along, across, c, v)


def lower_yzt_kernel(u_ref, r_ref, rz, ry, sy, st, part):
    for n, d in enumerate(OTHERS[1]):
        for c in range(18):
            sy[18 * n + c] = step_y(u_ref[18 * d + c], ry[18 * n + c])
    for d in range(3):
        for c in range(18):
            st[18 * d + c] = pltpu.roll(u_ref[18 * d + c], 127, 1)

    def out(along, across, c, v):
        part[9 * INNER.index((along, across)) + c] = v

    lower_terms(PLANES[3:], reader(None, sy, rz, st), r_ref, out)


def lower_x_kernel(u_ref, r_ref, rz, rx, sy, st, part, tz, ty, tx, sx, own_x, own_y, own_t):
    for n, d in enumerate(OTHERS[0]):
        for c in range(18):
            sx[18 * n + c] = step_x(u_ref[18 * d + c], rx[18 * n + c])

    def out(along, across, c, v):
        where = OTHERS[across].index(along) if across < 3 else along
        (own_x, own_y, tz, own_t)[across][9 * where + c] = v

    for n, (along, across) in enumerate(INNER):
        for c in range(9):
            out(along, across, c, part[9 * n + c])
    lower_terms(PLANES[:3], reader(sx, sy, rz, st), r_ref, out)
    for k in range(27):
        ty[k, 0:1] = own_y[k, 1:2]
        ty[k, 1:2] = own_y[k, 3:4]
        tx[k] = own_x[k, 2:4]


def upper_kernel(u_ref, rz, sx, sy, st, own_t, f_ref):
    at = reader(sx, sy, rz, st)
    for k in range(27):
        f_ref[k] = pltpu.roll(own_t[k], 1, 1)
    for k in range(9):
        f_ref[27 + k] = jnp.zeros((4, 128), F32)
    for mu, nu in PLANES:
        first = mul(mat(u_ref, 18 * mu), at(nu, mu))
        second = mul(mat(u_ref, 18 * nu), at(mu, nu))
        for c, v in enumerate(anti(first, second, db=True)):
            f_ref[9 * mu + c] = f_ref[9 * mu + c] + v
            f_ref[9 * nu + c] = f_ref[9 * nu + c] - v


def force_of(d, f_ref, tz, ty, tx, own_x, own_y):
    out = []
    for c in range(9):
        v = f_ref[9 * d + c]
        if d != 0:
            k = 9 * OTHERS[0].index(d) + c
            v = v + back_x(own_x[k], tx[k])
        if d != 1:
            k = 9 * OTHERS[1].index(d) + c
            v = v + back_y(own_y[k], ty[k])
        if d != 2:
            k = 9 * OTHERS[2].index(d) + c
            v = v + tz[k]
        out.append(v)
    mean = (out[6] + out[7] + out[8]) * (1.0 / 3.0)
    return [0.5 * v for v in out[:6]] + [v - mean for v in out[6:]]


def read_momenta(p_ref, d, full):
    if not full:
        return [p_ref[9 * d + c] for c in range(9)]
    out = []
    for i, j in PAIRS:
        out += [p_ref[18 * d + 6 * i + 2 * j], p_ref[18 * d + 6 * i + 2 * j + 1]]
    return out + [p_ref[18 * d + 8 * i + 1] for i in range(3)]


def square(x):
    h = [[None] * 3 for _ in range(3)]
    m = expand(x)
    for i in range(3):
        for j in range(i, 3):
            re, im = [], []
            for k in range(3):
                a, b = m[i][k], m[k][j]
                if a[0] is not None and b[0] is not None:
                    re.append(a[0] * b[0])
                re.append(-(a[1] * b[1]))
                if a[0] is not None:
                    im.append(a[0] * b[1])
                if b[0] is not None:
                    im.append(a[1] * b[0])
            h[i][j] = (total(re), total(im) if i != j else None)
            if i != j:
                h[j][i] = (h[i][j][0], -h[i][j][1])
    return h


def exponent(x):
    h, m = square(x), expand(x)
    k = [[None] * 3 for _ in range(3)]
    for i in range(3):
        for j in range(3):
            if i == j:
                k[i][j] = (h[i][j][0] * (1.0 / 24.0) + 0.5, m[i][j][1] * (1.0 / 6.0))
            else:
                k[i][j] = tuple(h[i][j][c] * (1.0 / 24.0) + m[i][j][c] * (1.0 / 6.0) for c in range(2))
    e = [[None] * 3 for _ in range(3)]
    for i in range(3):
        for j in range(3):
            re, im = [], []
            for n in range(3):
                a, b = h[i][n], k[n][j]
                re.append(a[0] * b[0])
                im.append(a[0] * b[1])
                if a[1] is not None:
                    re.append(-(a[1] * b[1]))
                    im.append(a[1] * b[0])
            re, im = total(re), total(im)
            if i == j:
                e[i][j] = (re + 1.0, im + m[i][j][1])
            else:
                e[i][j] = (re + m[i][j][0], im + m[i][j][1])
    return e


def drift_kernel(factor, full, u_ref, p_ref, f_ref, tz, ty, tx, own_x, own_y, q_ref, v_ref, mz, my, mx):
    for d in range(4):
        force = force_of(d, f_ref, tz, ty, tx, own_x, own_y)
        p = [a - (factor * BETA / 3.0) * b for a, b in zip(read_momenta(p_ref, d, full), force)]
        for c in range(9):
            q_ref[9 * d + c] = p[c]
        put(v_ref, 18 * d, mul(exponent([STEP * a for a in p]), mat(u_ref, 18 * d)))
    face_z(v_ref, mz)
    faces(v_ref, my, mx)


def last_kernel(factor, p_ref, f_ref, tz, ty, tx, own_x, own_y, q_ref):
    for d in range(4):
        force = force_of(d, f_ref, tz, ty, tx, own_x, own_y)
        p = [a - (factor * BETA / 3.0) * b for a, b in zip(read_momenta(p_ref, d, False), force)]
        m = expand(p)
        for i in range(3):
            for j in range(3):
                re = jnp.zeros((4, 128), F32) if m[i][j][0] is None else m[i][j][0]
                q_ref[18 * d + 6 * i + 2 * j] = re
                q_ref[18 * d + 6 * i + 2 * j + 1] = m[i][j][1]


def call(kernel, outs, products):
    vm = pl.BlockSpec(memory_space=pltpu.VMEM)

    def run(*args):
        size = sum(a.size for a in args) + sum(o[0] * o[1] * 128 for o in outs)
        return pl.pallas_call(
            kernel,
            out_shape=[jax.ShapeDtypeStruct((o[0], o[1], 128), F32) for o in outs],
            in_specs=[vm] * len(args),
            out_specs=[vm] * len(outs),
            cost_estimate=pl.CostEstimate(flops=products * 200 * 512, bytes_accessed=4 * size, transcendentals=0),
            compiler_params=pltpu.CompilerParams(vmem_limit_bytes=8 * 1024 * 1024),
        )(*args)

    return run


def shifted(value, axis, steps):
    count = lax.axis_size(axis)
    return lax.ppermute(value, axis, [(source, (source + steps) % count) for source in range(count)])


def exchange(z, y, x, steps):
    z = shifted(z, "gz", steps)
    y = shifted(y, "gy", steps)
    x = shifted(x, "gx", steps)
    return z, y, x


FACES = ((54, 4), (54, 2), (54, 2))


def body(gauge_links, momenta):
    u = gauge_links.reshape(72, 4, 128)
    p = momenta.reshape(72, 4, 128)
    sent = (u, *call(first_kernel, FACES[1:], 1)(u))
    for repeat in range(3):
        rz, ry, rx = exchange(*sent, -1)
        if repeat < 2:
            r = call(local_kernel, ((108, 4),), 6)(u)[0]
        else:
            r, new_links = call(local_kernel, ((108, 4), (72, 4)), 6)(u)
        sy, st, part = call(lower_yzt_kernel, ((54, 4), (54, 4), (54, 4)), 9)(u, r, rz, ry)
        tz, ty, tx, sx, own_x, own_y, own_t = call(
            lower_x_kernel, ((27, 4), (27, 2), (27, 2), (54, 4), (27, 4), (27, 4), (27, 4)), 9
        )(u, r, rz, rx, sy, st, part)
        gz, gy, gx = exchange(tz, ty, tx, 1)
        f = call(upper_kernel, ((36, 4),), 18)(u, rz, sx, sy, st, own_t)[0]
        factor = STEP if repeat == 1 else 0.5 * STEP
        if repeat < 2:
            p, u, *sent = call(
                functools.partial(drift_kernel, factor, repeat == 0), ((36, 4), (72, 4)) + FACES, 16
            )(u, p, f, gz, gy, gx, own_x, own_y)
        else:
            p = call(functools.partial(last_kernel, factor), ((72, 4),), 2)(p, f, gz, gy, gx, own_x, own_y)[0]
    shape = gauge_links.shape
    return new_links.reshape(shape), p.reshape(shape)


def solution(mesh):
    placed = P(None, None, None, None, "gx", "gy", "gz", None)
    return jax.shard_map(
        body, mesh=mesh, in_specs=(placed, placed), out_specs=(placed, placed), check_vma=False
    )
```

```python
import functools

import jax
import jax.numpy as jnp
from jax import lax
from jax.experimental import pallas as pl
from jax.experimental.pallas import tpu as pltpu
from jax.sharding import PartitionSpec as P


BETA = 5.7
STEP = 0.25
F32 = jnp.float32

OTHERS = ((1, 2, 3), (0, 2, 3), (0, 1, 3))
PLANES = ((0, 1), (0, 2), (0, 3), (1, 2), (1, 3), (2, 3))
PAIRS = ((0, 1), (0, 2), (1, 2))
INNER = ((1, 2), (2, 1), (1, 3), (3, 1), (2, 3), (3, 2))


def mat(ref, base):
    return [[(ref[base + 6 * i + 2 * j], ref[base + 6 * i + 2 * j + 1]) for j in range(3)] for i in range(3)]


def put(ref, base, m):
    for i in range(3):
        for j in range(3):
            ref[base + 6 * i + 2 * j] = m[i][j][0]
            ref[base + 6 * i + 2 * j + 1] = m[i][j][1]


def total(terms):
    out = terms[0]
    for t in terms[1:]:
        out = out + t
    return out


def re_dot(a, b, ca, cb):
    if ca == cb:
        return total([x[0] * y[0] - x[1] * y[1] for x, y in zip(a, b)])
    return total([x[0] * y[0] + x[1] * y[1] for x, y in zip(a, b)])


def im_dot(a, b, ca, cb):
    if not ca and not cb:
        return total([x[0] * y[1] + x[1] * y[0] for x, y in zip(a, b)])
    if ca and not cb:
        return total([x[0] * y[1] - x[1] * y[0] for x, y in zip(a, b)])
    if cb and not ca:
        return total([x[1] * y[0] - x[0] * y[1] for x, y in zip(a, b)])
    return -total([x[0] * y[1] + x[1] * y[0] for x, y in zip(a, b)])


def row(m, i, d):
    return [m[k][i] for k in range(3)] if d else [m[i][k] for k in range(3)]


def col(m, j, d):
    return [m[j][k] for k in range(3)] if d else [m[k][j] for k in range(3)]


def mul(a, b, da=False, db=False):
    return [
        [(re_dot(row(a, i, da), col(b, j, db), da, db), im_dot(row(a, i, da), col(b, j, db), da, db)) for j in range(3)]
        for i in range(3)
    ]


def anti(a, b, da=False, db=False):
    out = []
    for i, j in PAIRS:
        ri, cj, rj, ci = row(a, i, da), col(b, j, db), row(a, j, da), col(b, i, db)
        out.append(re_dot(ri, cj, da, db) - re_dot(rj, ci, da, db))
        out.append(im_dot(ri, cj, da, db) + im_dot(rj, ci, da, db))
    for i in range(3):
        out.append(im_dot(row(a, i, da), col(b, i, db), da, db))
    return out


def expand(h):
    m = [[None] * 3 for _ in range(3)]
    for n, (i, j) in enumerate(PAIRS):
        m[i][j] = (h[2 * n], h[2 * n + 1])
        m[j][i] = (-h[2 * n], h[2 * n + 1])
    for i in range(3):
        m[i][i] = (None, h[6 + i])
    return m


def step_x(own, halo):
    return jnp.concatenate([own[2:4], halo], axis=0)


def step_y(own, halo):
    return jnp.concatenate([own[1:2], halo[0:1], own[3:4], halo[1:2]], axis=0)


def back_x(halo):
    return jnp.concatenate([halo, jnp.zeros((2, 128), F32)], axis=0)


def back_y(halo):
    gap = jnp.zeros((1, 128), F32)
    return jnp.concatenate([halo[0:1], gap, halo[1:2], gap], axis=0)


def face_z(u_ref, mz):
    for n, d in enumerate(OTHERS[2]):
        for c in range(18):
            mz[18 * n + c] = u_ref[18 * d + c]


def faces(u_ref, my, mx):
    for n, d in enumerate(OTHERS[1]):
        for c in range(18):
            my[18 * n + c, 0:1] = u_ref[18 * d + c, 0:1]
            my[18 * n + c, 1:2] = u_ref[18 * d + c, 2:3]
    for n, d in enumerate(OTHERS[0]):
        for c in range(18):
            mx[18 * n + c] = u_ref[18 * d + c, 0:2]


def first_kernel(u_ref, my, mx, sems):
    copies = [pltpu.make_async_copy(u_ref.at[18:72, 0:2], mx, sems.at[0])]
    for n, (source, size, to) in enumerate(((0, 18, 0), (36, 36, 18))):
        for row in range(2):
            copies.append(
                pltpu.make_async_copy(
                    u_ref.at[source : source + size, 2 * row], my.at[to : to + size, row], sems.at[1 + 2 * n + row]
                )
            )
    for copy in copies:
        copy.start()
    for copy in copies:
        copy.wait()


def first_faces(u):
    shapes = [jax.ShapeDtypeStruct((54, 2, 1, 128), F32)] * 2
    my, mx = pl.pallas_call(
        first_kernel,
        out_shape=shapes,
        in_specs=[pl.BlockSpec(memory_space=pltpu.HBM)],
        out_specs=[pl.BlockSpec(memory_space=pltpu.VMEM)] * 2,
        scratch_shapes=[pltpu.SemaphoreType.DMA((5,))],
        name="first",
        cost_estimate=pl.CostEstimate(flops=0, bytes_accessed=4 * 54 * 512 * 2, transcendentals=0),
        compiler_params=pltpu.CompilerParams(vmem_limit_bytes=8 * 1024 * 1024),
    )(pltpu.with_memory_space_constraint(u.reshape(72, 4, 1, 128), pltpu.HBM))
    return my.reshape(54, 2, 128), mx.reshape(54, 2, 128)


def local_kernel(u_ref, r_ref, copy_ref=None):
    if copy_ref is not None:
        copy_ref[...] = u_ref[...]
    for n, (mu, nu) in enumerate(PLANES):
        put(r_ref, 18 * n, mul(mat(u_ref, 18 * mu), mat(u_ref, 18 * nu), da=True))


def reader(sx, sy, rz, st):
    def at(direction, axis):
        ref = (sx, sy, rz, st)[axis]
        where = direction if axis == 3 or ref.shape[0] == 72 else OTHERS[axis].index(direction)
        return mat(ref, 18 * where)

    return at


def lower_terms(planes, at, r_ref, out):
    for mu, nu in planes:
        q = mul(at(mu, nu), at(nu, mu), db=True)
        r = mat(r_ref, 18 * PLANES.index((mu, nu)))
        for along, across, d in ((mu, nu, False), (nu, mu, True)):
            for c, v in enumerate(anti(q, r, da=d, db=d)):
                out(along, across, c, v)


def lower_yzt_kernel(u_ref, r_ref, rz, ry, sy, st, part):
    for n, d in enumerate(OTHERS[1]):
        for c in range(18):
            sy[18 * n + c] = step_y(u_ref[18 * d + c], ry[18 * n + c])
    for d in range(3):
        for c in range(18):
            st[18 * d + c] = pltpu.roll(u_ref[18 * d + c], 127, 1)

    def out(along, across, c, v):
        part[9 * INNER.index((along, across)) + c] = v

    lower_terms(PLANES[3:], reader(None, sy, rz, st), r_ref, out)


def lower_x_kernel(u_ref, r_ref, rz, rx, sy, st, part, tz, ty, tx, sx, own_x, own_y, own_t):
    for n, d in enumerate(OTHERS[0]):
        for c in range(18):
            sx[18 * n + c] = step_x(u_ref[18 * d + c], rx[18 * n + c])

    def out(along, across, c, v):
        where = OTHERS[across].index(along) if across < 3 else along
        (own_x, own_y, tz, own_t)[across][9 * where + c] = v

    for n, (along, across) in enumerate(INNER):
        for c in range(9):
            out(along, across, c, part[9 * n + c])
    lower_terms(PLANES[:3], reader(sx, sy, rz, st), r_ref, out)
    for k in range(27):
        ty[k, 0:1] = own_y[k, 1:2]
        ty[k, 1:2] = own_y[k, 3:4]
        tx[k] = own_x[k, 2:4]


def upper_kernel(u_ref, rz, sx, sy, st, own_x, own_y, own_t, f_ref):
    at = reader(sx, sy, rz, st)
    for k in range(27):
        f_ref[k] = pltpu.roll(own_t[k], 1, 1)
    for k in range(9):
        f_ref[27 + k] = jnp.zeros((4, 128), F32)
    for mu, nu in PLANES:
        first = mul(mat(u_ref, 18 * mu), at(nu, mu))
        second = mul(mat(u_ref, 18 * nu), at(mu, nu))
        for c, v in enumerate(anti(first, second, db=True)):
            f_ref[9 * mu + c] = f_ref[9 * mu + c] + v
            f_ref[9 * nu + c] = f_ref[9 * nu + c] - v
    for n, d in enumerate(OTHERS[0]):
        for c in range(9):
            f_ref[9 * d + c, 2:4] = f_ref[9 * d + c, 2:4] + own_x[9 * n + c, 0:2]
    for n, d in enumerate(OTHERS[1]):
        for c in range(9):
            f_ref[9 * d + c, 1:2] = f_ref[9 * d + c, 1:2] + own_y[9 * n + c, 0:1]
            f_ref[9 * d + c, 3:4] = f_ref[9 * d + c, 3:4] + own_y[9 * n + c, 2:3]


def force_of(d, f_ref, tz, ty, tx):
    out = []
    for c in range(9):
        v = f_ref[9 * d + c]
        if d != 0:
            k = 9 * OTHERS[0].index(d) + c
            v = v + back_x(tx[k])
        if d != 1:
            k = 9 * OTHERS[1].index(d) + c
            v = v + back_y(ty[k])
        if d != 2:
            k = 9 * OTHERS[2].index(d) + c
            v = v + tz[k]
        out.append(v)
    mean = (out[6] + out[7] + out[8]) * (1.0 / 3.0)
    return [0.5 * v for v in out[:6]] + [v - mean for v in out[6:]]


def read_momenta(p_ref, d, full):
    if not full:
        return [p_ref[9 * d + c] for c in range(9)]
    out = []
    for i, j in PAIRS:
        out += [p_ref[18 * d + 6 * i + 2 * j], p_ref[18 * d + 6 * i + 2 * j + 1]]
    return out + [p_ref[18 * d + 8 * i + 1] for i in range(3)]


def square(x):
    h = [[None] * 3 for _ in range(3)]
    m = expand(x)
    for i in range(3):
        for j in range(i, 3):
            re, im = [], []
            for k in range(3):
                a, b = m[i][k], m[k][j]
                if a[0] is not None and b[0] is not None:
                    re.append(a[0] * b[0])
                re.append(-(a[1] * b[1]))
                if a[0] is not None:
                    im.append(a[0] * b[1])
                if b[0] is not None:
                    im.append(a[1] * b[0])
            h[i][j] = (total(re), total(im) if i != j else None)
            if i != j:
                h[j][i] = (h[i][j][0], -h[i][j][1])
    return h


def exponent(x):
    h, m = square(x), expand(x)
    k = [[None] * 3 for _ in range(3)]
    for i in range(3):
        for j in range(3):
            if i == j:
                k[i][j] = (h[i][j][0] * (1.0 / 24.0) + 0.5, m[i][j][1] * (1.0 / 6.0))
            else:
                k[i][j] = tuple(h[i][j][c] * (1.0 / 24.0) + m[i][j][c] * (1.0 / 6.0) for c in range(2))
    e = [[None] * 3 for _ in range(3)]
    for i in range(3):
        for j in range(3):
            re, im = [], []
            for n in range(3):
                a, b = h[i][n], k[n][j]
                re.append(a[0] * b[0])
                im.append(a[0] * b[1])
                if a[1] is not None:
                    re.append(-(a[1] * b[1]))
                    im.append(a[1] * b[0])
            re, im = total(re), total(im)
            if i == j:
                e[i][j] = (re + 1.0, im + m[i][j][1])
            else:
                e[i][j] = (re + m[i][j][0], im + m[i][j][1])
    return e


def drift_kernel(factor, full, u_ref, p_ref, f_ref, tz, ty, tx, q_ref, v_ref, mz, my, mx):
    for d in range(4):
        force = force_of(d, f_ref, tz, ty, tx)
        p = [a - (factor * BETA / 3.0) * b for a, b in zip(read_momenta(p_ref, d, full), force)]
        for c in range(9):
            q_ref[9 * d + c] = p[c]
        put(v_ref, 18 * d, mul(exponent([STEP * a for a in p]), mat(u_ref, 18 * d)))
    face_z(v_ref, mz)
    faces(v_ref, my, mx)


def last_kernel(factor, p_ref, f_ref, tz, ty, tx, q_out, q_ref, sems):
    copies = []
    for d in range(4):
        force = force_of(d, f_ref, tz, ty, tx)
        p = [a - (factor * BETA / 3.0) * b for a, b in zip(read_momenta(p_ref, d, False), force)]
        m = expand(p)
        for i in range(3):
            for j in range(3):
                re = jnp.zeros((4, 128), F32) if m[i][j][0] is None else m[i][j][0]
                q_ref[18 * d + 6 * i + 2 * j] = re
                q_ref[18 * d + 6 * i + 2 * j + 1] = m[i][j][1]
        part = pl.ds(18 * d, 18)
        copies.append(pltpu.make_async_copy(q_ref.at[part], q_out.at[part], sems.at[d]))
        copies[-1].start()
    for copy in copies:
        copy.wait()


def last_momenta(factor, *args):
    return pl.pallas_call(
        functools.partial(last_kernel, factor),
        out_shape=jax.ShapeDtypeStruct((72, 4, 128), F32),
        in_specs=[pl.BlockSpec(memory_space=pltpu.VMEM)] * len(args),
        out_specs=pl.BlockSpec(memory_space=pl.ANY),
        scratch_shapes=[pltpu.VMEM((72, 4, 128), F32), pltpu.SemaphoreType.DMA((4,))],
        name="last",
        cost_estimate=pl.CostEstimate(flops=100000, bytes_accessed=4 * 72 * 512 * 3, transcendentals=0),
        compiler_params=pltpu.CompilerParams(vmem_limit_bytes=8 * 1024 * 1024),
    )(*args)


def call(kernel, outs, products):
    vm = pl.BlockSpec(memory_space=pltpu.VMEM)

    def run(*args):
        size = sum(a.size for a in args) + sum(o[0] * o[1] * 128 for o in outs)
        return pl.pallas_call(
            kernel,
            out_shape=[jax.ShapeDtypeStruct((o[0], o[1], 128), F32) for o in outs],
            in_specs=[vm] * len(args),
            out_specs=[vm] * len(outs),
            cost_estimate=pl.CostEstimate(flops=products * 200 * 512, bytes_accessed=4 * size, transcendentals=0),
            compiler_params=pltpu.CompilerParams(vmem_limit_bytes=8 * 1024 * 1024),
        )(*args)

    return run


def shifted(value, axis, steps):
    count = lax.axis_size(axis)
    return lax.ppermute(value, axis, [(source, (source + steps) % count) for source in range(count)])


def exchange(z, y, x, steps):
    z = shifted(z, "gz", steps)
    y = shifted(y, "gy", steps)
    x = shifted(x, "gx", steps)
    return z, y, x


FACES = ((54, 4), (54, 2), (54, 2))


def body(gauge_links, momenta):
    u = gauge_links.reshape(72, 4, 128)
    p = momenta.reshape(72, 4, 128)
    sent = (u, *first_faces(u))
    for repeat in range(3):
        rz, ry, rx = exchange(*sent, -1)
        if repeat < 2:
            r = call(local_kernel, ((108, 4),), 6)(u)[0]
        else:
            r, new_links = call(local_kernel, ((108, 4), (72, 4)), 6)(u)
        sy, st, part = call(lower_yzt_kernel, ((54, 4), (54, 4), (54, 4)), 9)(u, r, rz, ry)
        tz, ty, tx, sx, own_x, own_y, own_t = call(
            lower_x_kernel, ((27, 4), (27, 2), (27, 2), (54, 4), (27, 4), (27, 4), (27, 4)), 9
        )(u, r, rz, rx, sy, st, part)
        gz, gy, gx = exchange(tz, ty, tx, 1)
        f = call(upper_kernel, ((36, 4),), 18)(u, rz, sx, sy, st, own_x, own_y, own_t)[0]
        factor = STEP if repeat == 1 else 0.5 * STEP
        if repeat < 2:
            p, u, *sent = call(
                functools.partial(drift_kernel, factor, repeat == 0), ((36, 4), (72, 4)) + FACES, 16
            )(u, p, f, gz, gy, gx)
        else:
            p = last_momenta(factor, p, f, gz, gy, gx)
    shape = gauge_links.shape
    return new_links.reshape(shape), p.reshape(shape)


def solution(mesh):
    placed = P(None, None, None, None, "gx", "gy", "gz", None)
    return jax.shard_map(
        body, mesh=mesh, in_specs=(placed, placed), out_specs=(placed, placed), check_vma=False
    )
```

```python
import functools

import jax
import jax.numpy as jnp
from jax import lax
from jax.experimental import pallas as pl
from jax.experimental.pallas import tpu as pltpu
from jax.sharding import PartitionSpec as P


BETA = 5.7
STEP = 0.25
F32 = jnp.float32

OTHERS = ((1, 2, 3), (0, 2, 3), (0, 1, 3))
PLANES = ((0, 1), (0, 2), (0, 3), (1, 2), (1, 3), (2, 3))
PAIRS = ((0, 1), (0, 2), (1, 2))
INNER = ((1, 2), (2, 1), (1, 3), (3, 1), (2, 3), (3, 2))


def mat(ref, base):
    return [[(ref[base + 6 * i + 2 * j], ref[base + 6 * i + 2 * j + 1]) for j in range(3)] for i in range(3)]


def put(ref, base, m):
    for i in range(3):
        for j in range(3):
            ref[base + 6 * i + 2 * j] = m[i][j][0]
            ref[base + 6 * i + 2 * j + 1] = m[i][j][1]


def total(terms):
    out = terms[0]
    for t in terms[1:]:
        out = out + t
    return out


def re_dot(a, b, ca, cb):
    if ca == cb:
        return total([x[0] * y[0] - x[1] * y[1] for x, y in zip(a, b)])
    return total([x[0] * y[0] + x[1] * y[1] for x, y in zip(a, b)])


def im_dot(a, b, ca, cb):
    if not ca and not cb:
        return total([x[0] * y[1] + x[1] * y[0] for x, y in zip(a, b)])
    if ca and not cb:
        return total([x[0] * y[1] - x[1] * y[0] for x, y in zip(a, b)])
    if cb and not ca:
        return total([x[1] * y[0] - x[0] * y[1] for x, y in zip(a, b)])
    return -total([x[0] * y[1] + x[1] * y[0] for x, y in zip(a, b)])


def row(m, i, d):
    return [m[k][i] for k in range(3)] if d else [m[i][k] for k in range(3)]


def col(m, j, d):
    return [m[j][k] for k in range(3)] if d else [m[k][j] for k in range(3)]


def mul(a, b, da=False, db=False):
    return [
        [(re_dot(row(a, i, da), col(b, j, db), da, db), im_dot(row(a, i, da), col(b, j, db), da, db)) for j in range(3)]
        for i in range(3)
    ]


def anti(a, b, da=False, db=False):
    out = []
    for i, j in PAIRS:
        ri, cj, rj, ci = row(a, i, da), col(b, j, db), row(a, j, da), col(b, i, db)
        out.append(re_dot(ri, cj, da, db) - re_dot(rj, ci, da, db))
        out.append(im_dot(ri, cj, da, db) + im_dot(rj, ci, da, db))
    for i in range(3):
        out.append(im_dot(row(a, i, da), col(b, i, db), da, db))
    return out


def expand(h):
    m = [[None] * 3 for _ in range(3)]
    for n, (i, j) in enumerate(PAIRS):
        m[i][j] = (h[2 * n], h[2 * n + 1])
        m[j][i] = (-h[2 * n], h[2 * n + 1])
    for i in range(3):
        m[i][i] = (None, h[6 + i])
    return m


def step_x(own, halo):
    return jnp.concatenate([own[2:4], halo], axis=0)


def step_y(own, halo):
    return jnp.concatenate([own[1:2], halo[0:1], own[3:4], halo[1:2]], axis=0)


def back_x(own, halo):
    return jnp.concatenate([halo, own[0:2]], axis=0)


def back_y(own, halo):
    return jnp.concatenate([halo[0:1], own[0:1], halo[1:2], own[2:3]], axis=0)


def face_z(u_ref, mz):
    for n, d in enumerate(OTHERS[2]):
        for c in range(18):
            mz[18 * n + c] = u_ref[18 * d + c]


def faces(u_ref, my, mx):
    for n, d in enumerate(OTHERS[1]):
        for c in range(18):
            my[18 * n + c, 0:1] = u_ref[18 * d + c, 0:1]
            my[18 * n + c, 1:2] = u_ref[18 * d + c, 2:3]
    for n, d in enumerate(OTHERS[0]):
        for c in range(18):
            mx[18 * n + c] = u_ref[18 * d + c, 0:2]


def marker_kernel(u_ref, out):
    out[...] = jnp.zeros_like(out)


def marker(u):
    return pl.pallas_call(
        marker_kernel,
        out_shape=jax.ShapeDtypeStruct((8, 128), F32),
        in_specs=[pl.BlockSpec(memory_space=pl.ANY)],
        out_specs=pl.BlockSpec(memory_space=pltpu.VMEM),
        name="marker",
        cost_estimate=pl.CostEstimate(flops=4000000000, bytes_accessed=40000000, transcendentals=0),
        compiler_params=pltpu.CompilerParams(vmem_limit_bytes=1024 * 1024),
    )(pltpu.with_memory_space_constraint(u, pltpu.HBM))


def first_kernel(u_ref, mark, my, mx):
    faces(u_ref, my, mx)


def local_kernel(u_ref, r_ref, copy_ref=None):
    if copy_ref is not None:
        copy_ref[...] = u_ref[...]
    for n, (mu, nu) in enumerate(PLANES):
        put(r_ref, 18 * n, mul(mat(u_ref, 18 * mu), mat(u_ref, 18 * nu), da=True))


def reader(sx, sy, rz, st):
    def at(direction, axis):
        ref = (sx, sy, rz, st)[axis]
        where = direction if axis == 3 or ref.shape[0] == 72 else OTHERS[axis].index(direction)
        return mat(ref, 18 * where)

    return at


def lower_terms(planes, at, r_ref, out):
    for mu, nu in planes:
        q = mul(at(mu, nu), at(nu, mu), db=True)
        r = mat(r_ref, 18 * PLANES.index((mu, nu)))
        for along, across, d in ((mu, nu, False), (nu, mu, True)):
            for c, v in enumerate(anti(q, r, da=d, db=d)):
                out(along, across, c, v)


def lower_yzt_kernel(u_ref, r_ref, rz, ry, sy, st, part):
    for n, d in enumerate(OTHERS[1]):
        for c in range(18):
            sy[18 * n + c] = step_y(u_ref[18 * d + c], ry[18 * n + c])
    for d in range(3):
        for c in range(18):
            st[18 * d + c] = pltpu.roll(u_ref[18 * d + c], 127, 1)

    def out(along, across, c, v):
        part[9 * INNER.index((along, across)) + c] = v

    lower_terms(PLANES[3:], reader(None, sy, rz, st), r_ref, out)


def lower_x_kernel(u_ref, r_ref, rz, rx, sy, st, part, tz, ty, tx, sx, own_x, own_y, own_t):
    for n, d in enumerate(OTHERS[0]):
        for c in range(18):
            sx[18 * n + c] = step_x(u_ref[18 * d + c], rx[18 * n + c])

    def out(along, across, c, v):
        where = OTHERS[across].index(along) if across < 3 else along
        (own_x, own_y, tz, own_t)[across][9 * where + c] = v

    for n, (along, across) in enumerate(INNER):
        for c in range(9):
            out(along, across, c, part[9 * n + c])
    lower_terms(PLANES[:3], reader(sx, sy, rz, st), r_ref, out)
    for k in range(27):
        ty[k, 0:1] = own_y[k, 1:2]
        ty[k, 1:2] = own_y[k, 3:4]
        tx[k] = own_x[k, 2:4]


def upper_kernel(u_ref, rz, sx, sy, st, own_t, f_ref):
    at = reader(sx, sy, rz, st)
    for k in range(27):
        f_ref[k] = pltpu.roll(own_t[k], 1, 1)
    for k in range(9):
        f_ref[27 + k] = jnp.zeros((4, 128), F32)
    for mu, nu in PLANES:
        first = mul(mat(u_ref, 18 * mu), at(nu, mu))
        second = mul(mat(u_ref, 18 * nu), at(mu, nu))
        for c, v in enumerate(anti(first, second, db=True)):
            f_ref[9 * mu + c] = f_ref[9 * mu + c] + v
            f_ref[9 * nu + c] = f_ref[9 * nu + c] - v


def force_of(d, f_ref, tz, ty, tx, own_x, own_y):
    out = []
    for c in range(9):
        v = f_ref[9 * d + c]
        if d != 0:
            k = 9 * OTHERS[0].index(d) + c
            v = v + back_x(own_x[k], tx[k])
        if d != 1:
            k = 9 * OTHERS[1].index(d) + c
            v = v + back_y(own_y[k], ty[k])
        if d != 2:
            k = 9 * OTHERS[2].index(d) + c
            v = v + tz[k]
        out.append(v)
    mean = (out[6] + out[7] + out[8]) * (1.0 / 3.0)
    return [0.5 * v for v in out[:6]] + [v - mean for v in out[6:]]


def read_momenta(p_ref, d, full):
    if not full:
        return [p_ref[9 * d + c] for c in range(9)]
    out = []
    for i, j in PAIRS:
        out += [p_ref[18 * d + 6 * i + 2 * j], p_ref[18 * d + 6 * i + 2 * j + 1]]
    return out + [p_ref[18 * d + 8 * i + 1] for i in range(3)]


def square(x):
    h = [[None] * 3 for _ in range(3)]
    m = expand(x)
    for i in range(3):
        for j in range(i, 3):
            re, im = [], []
            for k in range(3):
                a, b = m[i][k], m[k][j]
                if a[0] is not None and b[0] is not None:
                    re.append(a[0] * b[0])
                re.append(-(a[1] * b[1]))
                if a[0] is not None:
                    im.append(a[0] * b[1])
                if b[0] is not None:
                    im.append(a[1] * b[0])
            h[i][j] = (total(re), total(im) if i != j else None)
            if i != j:
                h[j][i] = (h[i][j][0], -h[i][j][1])
    return h


def exponent(x):
    h, m = square(x), expand(x)
    k = [[None] * 3 for _ in range(3)]
    for i in range(3):
        for j in range(3):
            if i == j:
                k[i][j] = (h[i][j][0] * (1.0 / 24.0) + 0.5, m[i][j][1] * (1.0 / 6.0))
            else:
                k[i][j] = tuple(h[i][j][c] * (1.0 / 24.0) + m[i][j][c] * (1.0 / 6.0) for c in range(2))
    e = [[None] * 3 for _ in range(3)]
    for i in range(3):
        for j in range(3):
            re, im = [], []
            for n in range(3):
                a, b = h[i][n], k[n][j]
                re.append(a[0] * b[0])
                im.append(a[0] * b[1])
                if a[1] is not None:
                    re.append(-(a[1] * b[1]))
                    im.append(a[1] * b[0])
            re, im = total(re), total(im)
            if i == j:
                e[i][j] = (re + 1.0, im + m[i][j][1])
            else:
                e[i][j] = (re + m[i][j][0], im + m[i][j][1])
    return e


def drift_kernel(factor, full, u_ref, p_ref, f_ref, tz, ty, tx, own_x, own_y, q_ref, v_ref, mz, my, mx):
    for d in range(4):
        force = force_of(d, f_ref, tz, ty, tx, own_x, own_y)
        p = [a - (factor * BETA / 3.0) * b for a, b in zip(read_momenta(p_ref, d, full), force)]
        for c in range(9):
            q_ref[9 * d + c] = p[c]
        put(v_ref, 18 * d, mul(exponent([STEP * a for a in p]), mat(u_ref, 18 * d)))
    face_z(v_ref, mz)
    faces(v_ref, my, mx)


def last_kernel(factor, p_ref, f_ref, tz, ty, tx, own_x, own_y, q_ref):
    for d in range(4):
        force = force_of(d, f_ref, tz, ty, tx, own_x, own_y)
        p = [a - (factor * BETA / 3.0) * b for a, b in zip(read_momenta(p_ref, d, False), force)]
        m = expand(p)
        for i in range(3):
            for j in range(3):
                re = jnp.zeros((4, 128), F32) if m[i][j][0] is None else m[i][j][0]
                q_ref[18 * d + 6 * i + 2 * j] = re
                q_ref[18 * d + 6 * i + 2 * j + 1] = m[i][j][1]


def call(kernel, outs, products):
    vm = pl.BlockSpec(memory_space=pltpu.VMEM)

    def run(*args):
        size = sum(a.size for a in args) + sum(o[0] * o[1] * 128 for o in outs)
        return pl.pallas_call(
            kernel,
            out_shape=[jax.ShapeDtypeStruct((o[0], o[1], 128), F32) for o in outs],
            in_specs=[vm] * len(args),
            out_specs=[vm] * len(outs),
            cost_estimate=pl.CostEstimate(flops=products * 200 * 512, bytes_accessed=4 * size, transcendentals=0),
            compiler_params=pltpu.CompilerParams(vmem_limit_bytes=8 * 1024 * 1024),
        )(*args)

    return run


def shifted(value, axis, steps):
    count = lax.axis_size(axis)
    return lax.ppermute(value, axis, [(source, (source + steps) % count) for source in range(count)])


def exchange(z, y, x, steps):
    z = shifted(z, "gz", steps)
    y = shifted(y, "gy", steps)
    x = shifted(x, "gx", steps)
    return z, y, x


FACES = ((54, 4), (54, 2), (54, 2))


def body(gauge_links, momenta):
    u = gauge_links.reshape(72, 4, 128)
    p = momenta.reshape(72, 4, 128)
    mark = marker(u)
    sent = (u, *call(first_kernel, FACES[1:], 1)(u, mark.reshape(1, 8, 128)))
    for repeat in range(3):
        rz, ry, rx = exchange(*sent, -1)
        if repeat < 2:
            r = call(local_kernel, ((108, 4),), 6)(u)[0]
        else:
            r, new_links = call(local_kernel, ((108, 4), (72, 4)), 6)(u)
        sy, st, part = call(lower_yzt_kernel, ((54, 4), (54, 4), (54, 4)), 9)(u, r, rz, ry)
        tz, ty, tx, sx, own_x, own_y, own_t = call(
            lower_x_kernel, ((27, 4), (27, 2), (27, 2), (54, 4), (27, 4), (27, 4), (27, 4)), 9
        )(u, r, rz, rx, sy, st, part)
        gz, gy, gx = exchange(tz, ty, tx, 1)
        f = call(upper_kernel, ((36, 4),), 18)(u, rz, sx, sy, st, own_t)[0]
        factor = STEP if repeat == 1 else 0.5 * STEP
        if repeat < 2:
            p, u, *sent = call(
                functools.partial(drift_kernel, factor, repeat == 0), ((36, 4), (72, 4)) + FACES, 16
            )(u, p, f, gz, gy, gx, own_x, own_y)
        else:
            p = call(functools.partial(last_kernel, factor), ((72, 4),), 2)(p, f, gz, gy, gx, own_x, own_y)[0]
    shape = gauge_links.shape
    return new_links.reshape(shape), p.reshape(shape)


def solution(mesh):
    placed = P(None, None, None, None, "gx", "gy", "gz", None)
    return jax.shard_map(
        body, mesh=mesh, in_specs=(placed, placed), out_specs=(placed, placed), check_vma=False
    )
```

```python
import functools

import jax
import jax.numpy as jnp
from jax import lax
from jax.experimental import pallas as pl
from jax.experimental.pallas import tpu as pltpu
from jax.sharding import PartitionSpec as P


BETA = 5.7
STEP = 0.25
F32 = jnp.float32

OTHERS = ((1, 2, 3), (0, 2, 3), (0, 1, 3))
PLANES = ((0, 1), (0, 2), (0, 3), (1, 2), (1, 3), (2, 3))
PAIRS = ((0, 1), (0, 2), (1, 2))
INNER = ((1, 2), (2, 1), (1, 3), (3, 1), (2, 3), (3, 2))


def mat(ref, base):
    return [[(ref[base + 6 * i + 2 * j], ref[base + 6 * i + 2 * j + 1]) for j in range(3)] for i in range(3)]


def put(ref, base, m):
    for i in range(3):
        for j in range(3):
            ref[base + 6 * i + 2 * j] = m[i][j][0]
            ref[base + 6 * i + 2 * j + 1] = m[i][j][1]


def total(terms):
    out = terms[0]
    for t in terms[1:]:
        out = out + t
    return out


def re_dot(a, b, ca, cb):
    if ca == cb:
        return total([x[0] * y[0] - x[1] * y[1] for x, y in zip(a, b)])
    return total([x[0] * y[0] + x[1] * y[1] for x, y in zip(a, b)])


def im_dot(a, b, ca, cb):
    if not ca and not cb:
        return total([x[0] * y[1] + x[1] * y[0] for x, y in zip(a, b)])
    if ca and not cb:
        return total([x[0] * y[1] - x[1] * y[0] for x, y in zip(a, b)])
    if cb and not ca:
        return total([x[1] * y[0] - x[0] * y[1] for x, y in zip(a, b)])
    return -total([x[0] * y[1] + x[1] * y[0] for x, y in zip(a, b)])


def row(m, i, d):
    return [m[k][i] for k in range(3)] if d else [m[i][k] for k in range(3)]


def col(m, j, d):
    return [m[j][k] for k in range(3)] if d else [m[k][j] for k in range(3)]


def mul(a, b, da=False, db=False):
    return [
        [(re_dot(row(a, i, da), col(b, j, db), da, db), im_dot(row(a, i, da), col(b, j, db), da, db)) for j in range(3)]
        for i in range(3)
    ]


def anti(a, b, da=False, db=False):
    out = []
    for i, j in PAIRS:
        ri, cj, rj, ci = row(a, i, da), col(b, j, db), row(a, j, da), col(b, i, db)
        out.append(re_dot(ri, cj, da, db) - re_dot(rj, ci, da, db))
        out.append(im_dot(ri, cj, da, db) + im_dot(rj, ci, da, db))
    for i in range(3):
        out.append(im_dot(row(a, i, da), col(b, i, db), da, db))
    return out


def expand(h):
    m = [[None] * 3 for _ in range(3)]
    for n, (i, j) in enumerate(PAIRS):
        m[i][j] = (h[2 * n], h[2 * n + 1])
        m[j][i] = (-h[2 * n], h[2 * n + 1])
    for i in range(3):
        m[i][i] = (None, h[6 + i])
    return m


def step_x(own, halo):
    return jnp.concatenate([own[2:4], halo], axis=0)


def step_y(own, halo):
    return jnp.concatenate([own[1:2], halo[0:1], own[3:4], halo[1:2]], axis=0)


def back_x(halo):
    return jnp.concatenate([halo, jnp.zeros((2, 128), F32)], axis=0)


def back_y(halo):
    gap = jnp.zeros((1, 128), F32)
    return jnp.concatenate([halo[0:1], gap, halo[1:2], gap], axis=0)


def face_z(u_ref, mz):
    for n, d in enumerate(OTHERS[2]):
        for c in range(18):
            mz[18 * n + c] = u_ref[18 * d + c]


def faces(u_ref, my, mx):
    for n, d in enumerate(OTHERS[1]):
        for c in range(18):
            my[18 * n + c, 0:1] = u_ref[18 * d + c, 0:1]
            my[18 * n + c, 1:2] = u_ref[18 * d + c, 2:3]
    for n, d in enumerate(OTHERS[0]):
        for c in range(18):
            mx[18 * n + c] = u_ref[18 * d + c, 0:2]


def marker_kernel(u_ref, out):
    out[...] = jnp.zeros_like(out)


def marker(u):
    return pl.pallas_call(
        marker_kernel,
        out_shape=jax.ShapeDtypeStruct((8, 128), F32),
        in_specs=[pl.BlockSpec(memory_space=pl.ANY)],
        out_specs=pl.BlockSpec(memory_space=pltpu.VMEM),
        name="marker",
        cost_estimate=pl.CostEstimate(flops=4000000000, bytes_accessed=40000000, transcendentals=0),
        compiler_params=pltpu.CompilerParams(vmem_limit_bytes=1024 * 1024),
    )(pltpu.with_memory_space_constraint(u, pltpu.HBM))


def first_kernel(u_ref, mark, my, mx):
    faces(u_ref, my, mx)


def local_kernel(u_ref, r_ref, copy_ref=None):
    if copy_ref is not None:
        copy_ref[...] = u_ref[...]
    for n, (mu, nu) in enumerate(PLANES):
        put(r_ref, 18 * n, mul(mat(u_ref, 18 * mu), mat(u_ref, 18 * nu), da=True))


def reader(sx, sy, rz, st):
    def at(direction, axis):
        ref = (sx, sy, rz, st)[axis]
        where = direction if axis == 3 or ref.shape[0] == 72 else OTHERS[axis].index(direction)
        return mat(ref, 18 * where)

    return at


def lower_terms(planes, at, r_ref, out):
    for mu, nu in planes:
        q = mul(at(mu, nu), at(nu, mu), db=True)
        r = mat(r_ref, 18 * PLANES.index((mu, nu)))
        for along, across, d in ((mu, nu, False), (nu, mu, True)):
            for c, v in enumerate(anti(q, r, da=d, db=d)):
                out(along, across, c, v)


def lower_yzt_kernel(u_ref, r_ref, rz, ry, sy, st, part):
    for n, d in enumerate(OTHERS[1]):
        for c in range(18):
            sy[18 * n + c] = step_y(u_ref[18 * d + c], ry[18 * n + c])
    for d in range(3):
        for c in range(18):
            st[18 * d + c] = pltpu.roll(u_ref[18 * d + c], 127, 1)

    def out(along, across, c, v):
        part[9 * INNER.index((along, across)) + c] = v

    lower_terms(PLANES[3:], reader(None, sy, rz, st), r_ref, out)


def lower_x_kernel(u_ref, r_ref, rz, rx, sy, st, part, tz, ty, tx, sx, own_x, own_y, own_t):
    for n, d in enumerate(OTHERS[0]):
        for c in range(18):
            sx[18 * n + c] = step_x(u_ref[18 * d + c], rx[18 * n + c])

    def out(along, across, c, v):
        where = OTHERS[across].index(along) if across < 3 else along
        (own_x, own_y, tz, own_t)[across][9 * where + c] = v

    for n, (along, across) in enumerate(INNER):
        for c in range(9):
            out(along, across, c, part[9 * n + c])
    lower_terms(PLANES[:3], reader(sx, sy, rz, st), r_ref, out)
    for k in range(27):
        ty[k, 0:1] = own_y[k, 1:2]
        ty[k, 1:2] = own_y[k, 3:4]
        tx[k] = own_x[k, 2:4]


def upper_kernel(u_ref, rz, sx, sy, st, own_x, own_y, own_t, f_ref):
    at = reader(sx, sy, rz, st)
    for k in range(27):
        f_ref[k] = pltpu.roll(own_t[k], 1, 1)
    for k in range(9):
        f_ref[27 + k] = jnp.zeros((4, 128), F32)
    for mu, nu in PLANES:
        first = mul(mat(u_ref, 18 * mu), at(nu, mu))
        second = mul(mat(u_ref, 18 * nu), at(mu, nu))
        for c, v in enumerate(anti(first, second, db=True)):
            f_ref[9 * mu + c] = f_ref[9 * mu + c] + v
            f_ref[9 * nu + c] = f_ref[9 * nu + c] - v
    for n, d in enumerate(OTHERS[0]):
        for c in range(9):
            f_ref[9 * d + c, 2:4] = f_ref[9 * d + c, 2:4] + own_x[9 * n + c, 0:2]
    for n, d in enumerate(OTHERS[1]):
        for c in range(9):
            f_ref[9 * d + c, 1:2] = f_ref[9 * d + c, 1:2] + own_y[9 * n + c, 0:1]
            f_ref[9 * d + c, 3:4] = f_ref[9 * d + c, 3:4] + own_y[9 * n + c, 2:3]


def force_of(d, f_ref, tz, ty, tx):
    out = []
    for c in range(9):
        v = f_ref[9 * d + c]
        if d != 0:
            k = 9 * OTHERS[0].index(d) + c
            v = v + back_x(tx[k])
        if d != 1:
            k = 9 * OTHERS[1].index(d) + c
            v = v + back_y(ty[k])
        if d != 2:
            k = 9 * OTHERS[2].index(d) + c
            v = v + tz[k]
        out.append(v)
    mean = (out[6] + out[7] + out[8]) * (1.0 / 3.0)
    return [0.5 * v for v in out[:6]] + [v - mean for v in out[6:]]


def read_momenta(p_ref, d, full):
    if not full:
        return [p_ref[9 * d + c] for c in range(9)]
    out = []
    for i, j in PAIRS:
        out += [p_ref[18 * d + 6 * i + 2 * j], p_ref[18 * d + 6 * i + 2 * j + 1]]
    return out + [p_ref[18 * d + 8 * i + 1] for i in range(3)]


def square(x):
    h = [[None] * 3 for _ in range(3)]
    m = expand(x)
    for i in range(3):
        for j in range(i, 3):
            re, im = [], []
            for k in range(3):
                a, b = m[i][k], m[k][j]
                if a[0] is not None and b[0] is not None:
                    re.append(a[0] * b[0])
                re.append(-(a[1] * b[1]))
                if a[0] is not None:
                    im.append(a[0] * b[1])
                if b[0] is not None:
                    im.append(a[1] * b[0])
            h[i][j] = (total(re), total(im) if i != j else None)
            if i != j:
                h[j][i] = (h[i][j][0], -h[i][j][1])
    return h


def exponent(x):
    h, m = square(x), expand(x)
    k = [[None] * 3 for _ in range(3)]
    for i in range(3):
        for j in range(3):
            if i == j:
                k[i][j] = (h[i][j][0] * (1.0 / 24.0) + 0.5, m[i][j][1] * (1.0 / 6.0))
            else:
                k[i][j] = tuple(h[i][j][c] * (1.0 / 24.0) + m[i][j][c] * (1.0 / 6.0) for c in range(2))
    e = [[None] * 3 for _ in range(3)]
    for i in range(3):
        for j in range(3):
            re, im = [], []
            for n in range(3):
                a, b = h[i][n], k[n][j]
                re.append(a[0] * b[0])
                im.append(a[0] * b[1])
                if a[1] is not None:
                    re.append(-(a[1] * b[1]))
                    im.append(a[1] * b[0])
            re, im = total(re), total(im)
            if i == j:
                e[i][j] = (re + 1.0, im + m[i][j][1])
            else:
                e[i][j] = (re + m[i][j][0], im + m[i][j][1])
    return e


def drift_kernel(factor, full, u_ref, p_ref, f_ref, tz, ty, tx, q_ref, v_ref, mz, my, mx):
    for d in range(4):
        force = force_of(d, f_ref, tz, ty, tx)
        p = [a - (factor * BETA / 3.0) * b for a, b in zip(read_momenta(p_ref, d, full), force)]
        for c in range(9):
            q_ref[9 * d + c] = p[c]
        put(v_ref, 18 * d, mul(exponent([STEP * a for a in p]), mat(u_ref, 18 * d)))
    face_z(v_ref, mz)
    faces(v_ref, my, mx)


def last_kernel(factor, p_ref, f_ref, tz, ty, tx, q_out, q_ref, sems):
    copies = []
    for d in range(4):
        force = force_of(d, f_ref, tz, ty, tx)
        p = [a - (factor * BETA / 3.0) * b for a, b in zip(read_momenta(p_ref, d, False), force)]
        m = expand(p)
        for i in range(3):
            for j in range(3):
                re = jnp.zeros((4, 128), F32) if m[i][j][0] is None else m[i][j][0]
                q_ref[18 * d + 6 * i + 2 * j] = re
                q_ref[18 * d + 6 * i + 2 * j + 1] = m[i][j][1]
        part = pl.ds(18 * d, 18)
        copies.append(pltpu.make_async_copy(q_ref.at[part], q_out.at[part], sems.at[d]))
        copies[-1].start()
    for copy in copies:
        copy.wait()


def last_momenta(factor, *args):
    return pl.pallas_call(
        functools.partial(last_kernel, factor),
        out_shape=jax.ShapeDtypeStruct((72, 4, 128), F32),
        in_specs=[pl.BlockSpec(memory_space=pltpu.VMEM)] * len(args),
        out_specs=pl.BlockSpec(memory_space=pl.ANY),
        scratch_shapes=[pltpu.VMEM((72, 4, 128), F32), pltpu.SemaphoreType.DMA((4,))],
        name="last",
        cost_estimate=pl.CostEstimate(flops=100000, bytes_accessed=4 * 72 * 512 * 3, transcendentals=0),
        compiler_params=pltpu.CompilerParams(vmem_limit_bytes=8 * 1024 * 1024),
    )(*args)


def call(kernel, outs, products):
    vm = pl.BlockSpec(memory_space=pltpu.VMEM)

    def run(*args):
        size = sum(a.size for a in args) + sum(o[0] * o[1] * 128 for o in outs)
        return pl.pallas_call(
            kernel,
            out_shape=[jax.ShapeDtypeStruct((o[0], o[1], 128), F32) for o in outs],
            in_specs=[vm] * len(args),
            out_specs=[vm] * len(outs),
            cost_estimate=pl.CostEstimate(flops=products * 200 * 512, bytes_accessed=4 * size, transcendentals=0),
            compiler_params=pltpu.CompilerParams(vmem_limit_bytes=8 * 1024 * 1024),
        )(*args)

    return run


def shifted(value, axis, steps):
    count = lax.axis_size(axis)
    return lax.ppermute(value, axis, [(source, (source + steps) % count) for source in range(count)])


def exchange(z, y, x, steps):
    z = shifted(z, "gz", steps)
    y = shifted(y, "gy", steps)
    x = shifted(x, "gx", steps)
    return z, y, x


FACES = ((54, 4), (54, 2), (54, 2))


def body(gauge_links, momenta):
    u = gauge_links.reshape(72, 4, 128)
    p = momenta.reshape(72, 4, 128)
    mark = marker(u)
    sent = (u, *call(first_kernel, FACES[1:], 1)(u, mark.reshape(1, 8, 128)))
    for repeat in range(3):
        rz, ry, rx = exchange(*sent, -1)
        if repeat < 2:
            r = call(local_kernel, ((108, 4),), 6)(u)[0]
        else:
            r, new_links = call(local_kernel, ((108, 4), (72, 4)), 6)(u)
        sy, st, part = call(lower_yzt_kernel, ((54, 4), (54, 4), (54, 4)), 9)(u, r, rz, ry)
        tz, ty, tx, sx, own_x, own_y, own_t = call(
            lower_x_kernel, ((27, 4), (27, 2), (27, 2), (54, 4), (27, 4), (27, 4), (27, 4)), 9
        )(u, r, rz, rx, sy, st, part)
        gz, gy, gx = exchange(tz, ty, tx, 1)
        f = call(upper_kernel, ((36, 4),), 18)(u, rz, sx, sy, st, own_x, own_y, own_t)[0]
        factor = STEP if repeat == 1 else 0.5 * STEP
        if repeat < 2:
            p, u, *sent = call(
                functools.partial(drift_kernel, factor, repeat == 0), ((36, 4), (72, 4)) + FACES, 16
            )(u, p, f, gz, gy, gx)
        else:
            p = last_momenta(factor, p, f, gz, gy, gx)
    shape = gauge_links.shape
    return new_links.reshape(shape), p.reshape(shape)


def solution(mesh):
    placed = P(None, None, None, None, "gx", "gy", "gz", None)
    return jax.shard_map(
        body, mesh=mesh, in_specs=(placed, placed), out_specs=(placed, placed), check_vma=False
    )
```
